32 devices in a mesh: group: 4 (over y, core), member: 8 (over z, x).
Axes of the slice: x: 2, y: 2, z: 4, core: 2. Of those that a mesh axis runs over, the one named last changes fastest.
Arguments:
- features: bfloat16 [16384, 128], P(('group', 'member')), may hold values from -6 to 6
- edge_tiles: bfloat16 [8192, 128, 128], P(('group', 'member')), may hold values from -0.09375 to 0.09375
- tile_slot: int32 [32, 256], P(('group', 'member')), may hold values from 0 to 7
- tile_column: int32 [32, 256], P(('group', 'member')), may hold values from 0 to 31
- mirror_count: int32 [32, 4], P(('group', 'member')), may hold values from 0 to 2, as said below
- mirror_block: int32 [32, 4, 2], P(('group', 'member')), may hold values from 0 to 3, as said below
- weight_first: bfloat16 [128, 256], replicated, may hold values from -0.5 to 0.5
- bias_first: float32 [256], replicated, may hold values from -3 to 3
- weight_second: bfloat16 [256, 256], replicated, may hold values from -0.375 to 0.375
- bias_second: float32 [256], replicated, may hold values from -3 to 3
Outputs:
- layer_out: bfloat16 [16384, 256], P(('group', 'member'))
The draws below stay inside these ranges and needn't reach their ends.
Inputs may be any that keep to these rules, and one draw needn't show every extreme that they name: `mirror_count`: at most 2 live mirror slots of one device for one destination group. `mirror_block`: the 2 entries of one device and destination group are distinct.
All inputs are finite; a program needn't handle non-finite values.
Results may differ from the reference program's by a relative error of at most 0.01.
Values may be sent and summed in bfloat16 or wider, within the bound.
A program may use at most 64 MiB of HBM per device.

```python
import jax
import jax.numpy as jnp
from jax import lax

TILE = 128
F_IN = 128
HID = 256
BLK_DEV = 4
TILES_DEV = 256
SLOT_CAP = 2
NODES = 16384
DEVICES_ALL = 32
N_GROUP = 4
N_MEMBER = 8


def draw_mirror_count(key, part):
    device_total = N_GROUP * N_MEMBER
    extra = jax.random.randint(key, (device_total, N_GROUP), 0, SLOT_CAP + 1)
    first = (jnp.arange(N_GROUP) == 0)[None, :]
    return jnp.where(first, SLOT_CAP, extra).astype(jnp.int32)


def draw_mirror_block(key, part):
    device_total = N_GROUP * N_MEMBER
    scores = jax.random.randint(key, (device_total, N_GROUP, BLK_DEV), 0, 1048576)
    scores = scores * BLK_DEV + jnp.arange(BLK_DEV)[None, None, :]
    order = jnp.argsort(scores, axis=-1)
    return order[:, :, :SLOT_CAP].astype(jnp.int32)


def with_ends(drawn, own_key, smallest, largest):
    dims = drawn.shape
    index_at = [jax.random.randint(jax.random.fold_in(own_key, axis), (), 0, dims[axis]) for axis in range(len(dims))]
    drawn = drawn.at[tuple(index_at)].set(smallest)
    longest = dims.index(max(dims))
    index_at[longest] = (index_at[longest] + 1) % dims[longest]
    return drawn.at[tuple(index_at)].set(largest)


def level_of(key, extent, split, low, largest):
    def one(axis_at, blocks):
        heights = jax.random.uniform(jax.random.fold_in(jax.random.fold_in(key, 6), axis_at), (blocks,), jnp.float32, low / len(split), largest / len(split))
        return jnp.repeat(jnp.exp(heights), extent[axis_at] // blocks).reshape((-1,) + (1,) * (len(extent) - axis_at - 1))

    level = one(*split[0])
    for cut in split[1:]:
        level = level * one(*cut)
    return level


def scatter_about(own_key, extent, width, bound, shards=(), kind=jnp.bfloat16):
    gain = level_of(own_key, extent, shards, -0.22, 0.18) if shards else 1.0
    values = jax.random.normal(own_key, extent, jnp.float32) * width * gain
    return jnp.minimum(jnp.maximum(values, -bound), bound).astype(kind)


def setup_inputs(seed: int = 0) -> dict:
    splits = jax.random.split(jax.random.key(seed), 11)
    features = scatter_about(splits[0], (NODES, F_IN), 1.0, 6.0, ((0, 32),))
    edge_tiles = scatter_about(splits[1], (DEVICES_ALL * TILES_DEV, TILE, TILE), (TILE * TILES_DEV // 8) ** -0.5, 0.09375, ((0, 32),))
    tile_slot = with_ends(jax.random.randint(splits[2], (DEVICES_ALL, TILES_DEV), 0, N_GROUP * SLOT_CAP), jax.random.fold_in(splits[2], 1), 0, (N_GROUP * SLOT_CAP) - 1).astype(jnp.int32)
    tile_column = with_ends(jax.random.randint(splits[3], (DEVICES_ALL, TILES_DEV), 0, N_MEMBER * BLK_DEV), jax.random.fold_in(splits[3], 1), 0, (N_MEMBER * BLK_DEV) - 1).astype(jnp.int32)
    mirror_count = draw_mirror_count(jax.random.fold_in(splits[10], 71), 0)
    mirror_block = draw_mirror_block(jax.random.fold_in(splits[10], 71), 0)
    weight_first = scatter_about(splits[6], (F_IN, HID), F_IN ** -0.5, 0.5)
    bias_first = scatter_about(splits[7], (HID,), 0.5, 3.0, (), jnp.float32)
    weight_second = scatter_about(splits[8], (HID, HID), HID ** -0.5, 0.375)
    bias_second = scatter_about(splits[9], (HID,), 0.5, 3.0, (), jnp.float32)
    return dict(features=features, edge_tiles=edge_tiles, tile_slot=tile_slot, tile_column=tile_column, mirror_count=mirror_count, mirror_block=mirror_block, weight_first=weight_first, bias_first=bias_first, weight_second=weight_second, bias_second=bias_second)


def reference(features, edge_tiles, tile_slot, tile_column, mirror_count, mirror_block, weight_first, bias_first, weight_second, bias_second):
    device_total = N_GROUP * N_MEMBER
    slot_total = N_GROUP * SLOT_CAP
    device_ids = jnp.arange(device_total, dtype=jnp.int32)
    group_index = device_ids // N_MEMBER
    member_index = device_ids % N_MEMBER
    dest_group = (tile_slot // SLOT_CAP).astype(jnp.int32)
    within = (tile_slot % SLOT_CAP).astype(jnp.int32)
    slot_count = jnp.take_along_axis(mirror_count, dest_group, axis=1)
    alive_mask = (within < slot_count).astype(jnp.float32)
    sources = (group_index[:, None] * (N_MEMBER * BLK_DEV) + tile_column).astype(jnp.int32)
    slot_group = (jnp.arange(slot_total, dtype=jnp.int32) // SLOT_CAP).astype(jnp.int32)
    slot_targets = ((slot_group[None, :] * N_MEMBER + member_index[:, None]) * BLK_DEV + mirror_block.reshape(device_total, slot_total)).astype(jnp.int32)
    tile_grid = edge_tiles.reshape(device_total, TILES_DEV, TILE, TILE)

    def aggregate(node_rows):
        channels = node_rows.shape[1]
        block_rows = node_rows.reshape(-1, TILE, channels).astype(jnp.float32)

        def advance(totals, pieces):
            tile_set, slot_set, source_set, alive_set, target_set = pieces
            products = jnp.einsum("tij,tjf->tif", tile_set.astype(jnp.float32), block_rows[source_set], precision=lax.Precision.HIGHEST)
            products = products * alive_set[:, None, None]
            partial_value = jnp.zeros((slot_total, TILE, channels), jnp.float32).at[slot_set].add(products)
            partial_value = lax.optimization_barrier(partial_value.astype(jnp.bfloat16)).astype(jnp.float32)
            return totals.at[target_set].add(partial_value), None

        start = jnp.zeros(block_rows.shape, jnp.float32)
        totals, _ = lax.scan(advance, start, (tile_grid, tile_slot.astype(jnp.int32), sources, alive_mask, slot_targets))
        return totals.reshape(-1, channels)

    first_sum = aggregate(features).astype(jnp.bfloat16)
    hidden = jnp.maximum(jnp.dot(first_sum, weight_first, preferred_element_type=jnp.float32) + bias_first, 0.0).astype(jnp.bfloat16)
    second = aggregate(hidden).astype(jnp.bfloat16)
    return (jnp.dot(second, weight_second, preferred_element_type=jnp.float32) + bias_second).astype(jnp.bfloat16)
```

```python
import functools

import jax
import jax.numpy as jnp
from jax import lax
from jax.experimental import pallas as pl
from jax.experimental.pallas import tpu as pltpu
from jax.sharding import PartitionSpec as P

F32 = jnp.float32
BF16 = jnp.bfloat16


def kernel(
    n,
    groups,
    cap,
    keep,
    prev_ref,
    last_ref,
    feat_ref,
    tiles_ref,
    hot_ref,
    w1_ref,
    b1_ref,
    w2_ref,
    b2_ref,
    out_ref,
    tile_buf,
    run_buf,
    stage_buf,
    gather1,
    gather2,
    acc1,
    acc2,
    part1,
    part2,
    got1,
    got2,
    got_hot,
    own_sum,
    tile_sem,
    hot_send,
    hot_recv,
    ag1_send,
    ag1_recv,
    rs1_send,
    rs1_recv,
    ag2_send,
    ag2_recv,
    rs2_send,
    rs2_recv,
):
    me = lax.axis_index("member")
    g = lax.axis_index("group")
    total = tiles_ref.shape[0]
    size = tiles_ref.shape[1]
    rows = feat_ref.shape[0]
    blocks = rows // size
    slots = groups * cap
    columns = n * blocks
    pieces = tile_sem.shape[0]
    piece = total // pieces

    def tile_copy(i):
        span = pl.ds(i * piece, piece)
        return pltpu.make_async_copy(tiles_ref.at[span], tile_buf.at[span], tile_sem.at[i])

    def member_copy(src, bank, k, send, recv):
        return pltpu.make_async_remote_copy(
            src_ref=src,
            dst_ref=bank.at[me],
            send_sem=send.at[k],
            recv_sem=recv.at[k],
            device_id={"member": lax.rem(me + k, n)},
            device_id_type=pl.DeviceIdType.MESH,
        )

    def member_arrival(src, bank, k, send, recv):
        origin = lax.rem(me + n - k, n)
        return pltpu.make_async_remote_copy(
            src_ref=src,
            dst_ref=bank.at[origin],
            send_sem=send.at[k],
            recv_sem=recv.at[k],
            device_id={"member": lax.rem(me + k, n)},
            device_id_type=pl.DeviceIdType.MESH,
        )

    def group_copy(bank, got, k, send, recv):
        to = lax.rem(g + k, groups)
        return pltpu.make_async_remote_copy(
            src_ref=bank.at[to],
            dst_ref=got.at[k],
            send_sem=send.at[k],
            recv_sem=recv.at[k],
            device_id={"group": to},
            device_id_type=pl.DeviceIdType.MESH,
        )

    for i in range(pieces):
        tile_copy(i).start()

    barrier = pltpu.get_barrier_semaphore()

    def greet_member(k, c):
        pl.semaphore_signal(
            barrier,
            inc=1,
            device_id={"member": lax.rem(me + k, n)},
            device_id_type=pl.DeviceIdType.MESH,
        )
        return c

    lax.fori_loop(1, n, greet_member, 0)
    for k in range(1, groups):
        pl.semaphore_signal(
            barrier,
            inc=1,
            device_id={"group": lax.rem(g + k, groups)},
            device_id_type=pl.DeviceIdType.MESH,
        )
    pl.semaphore_wait(barrier, n - 1 + groups - 1)

    def send_features(k, c):
        member_copy(feat_ref, gather1, k, ag1_send, ag1_recv).start()
        return c

    lax.fori_loop(1, n, send_features, 0)
    for k in range(1, groups):
        group_copy(hot_ref, got_hot, k, hot_send, hot_recv).start()

    gather1[me] = feat_ref[...]
    tile_buf[total] = jnp.zeros((size, size), BF16)
    run_buf[total] = jnp.zeros((size, size), F32)

    def chain(t, c):
        value = tile_buf[t].astype(F32) + run_buf[prev_ref[t]]
        run_buf[t] = value
        tile_buf[t] = value.astype(BF16)
        return c

    for i in range(pieces):
        tile_copy(i).wait()
        lax.fori_loop(i * piece, (i + 1) * piece, chain, 0)

    def stage(k, at):
        origin = lax.rem(me + n - k, n)
        for s in range(slots):
            for b in range(blocks):
                stage_buf[at, s * size : (s + 1) * size, b * size : (b + 1) * size] = tile_buf[
                    last_ref[s * columns + origin * blocks + b]
                ]

    if keep:

        def stage_all(k, c):
            stage(k, k)
            return c

        lax.fori_loop(0, n, stage_all, 0)

    def place(k):
        if keep:
            return k
        stage(k, 0)
        return 0

    def combine(part, got):
        sums = []
        for b in range(blocks):
            value = None
            for k in range(groups):
                hot = hot_ref[g] if k == 0 else got_hot[k]
                for c in range(cap):
                    block = (
                        part[g, c * size : (c + 1) * size, :]
                        if k == 0
                        else got[k, c * size : (c + 1) * size, :]
                    )
                    weight = hot[c * blocks + b : c * blocks + b + 1, :]
                    repeat = block.shape[1] // weight.shape[1]
                    if repeat > 1:
                        weight = jnp.concatenate([weight] * repeat, axis=1)
                    term = weight * block.astype(F32)
                    value = term if value is None else value + term
            sums.append(value.astype(BF16))
        return sums

    acc1[...] = jnp.dot(stage_buf[place(0)], feat_ref[...], preferred_element_type=F32)

    def first_layer(k, c):
        at = place(k)
        member_arrival(feat_ref, gather1, k, ag1_send, ag1_recv).wait_recv()
        origin = lax.rem(me + n - k, n)
        acc1[...] += jnp.dot(stage_buf[at], gather1[origin], preferred_element_type=F32)
        return c

    lax.fori_loop(1, n, first_layer, 0)
    for e in range(groups):
        part1[e] = acc1[e * cap * size : (e + 1) * cap * size, :].astype(BF16)
    for k in range(1, groups):
        group_copy(part1, got1, k, rs1_send, rs1_recv).start()
    for k in range(1, groups):
        group_copy(hot_ref, got_hot, k, hot_send, hot_recv).wait_recv()
    for k in range(1, groups):
        group_copy(part1, got1, k, rs1_send, rs1_recv).wait_recv()
    sums = combine(part1, got1)
    for b in range(blocks):
        own_sum[b * size : (b + 1) * size, :] = sums[b]

    def send_sums(k, c):
        member_copy(own_sum, gather2, k, ag2_send, ag2_recv).start()
        return c

    lax.fori_loop(1, n, send_sums, 0)

    def hidden_of(value):
        raw = jnp.dot(value, w1_ref[...], preferred_element_type=F32) + b1_ref[...]
        return jnp.maximum(raw, 0.0).astype(BF16)

    acc2[...] = jnp.dot(stage_buf[place(0)], hidden_of(own_sum[...]), preferred_element_type=F32)

    def second_layer(k, c):
        at = place(k)
        member_arrival(own_sum, gather2, k, ag2_send, ag2_recv).wait_recv()
        origin = lax.rem(me + n - k, n)
        acc2[...] += jnp.dot(
            stage_buf[at], hidden_of(gather2[origin]), preferred_element_type=F32
        )
        return c

    lax.fori_loop(1, n, second_layer, 0)
    for e in range(groups):
        part2[e] = acc2[e * cap * size : (e + 1) * cap * size, :].astype(BF16)
    for k in range(1, groups):
        group_copy(part2, got2, k, rs2_send, rs2_recv).start()

    def drain(k, c):
        member_copy(feat_ref, gather1, k, ag1_send, ag1_recv).wait_send()
        member_copy(own_sum, gather2, k, ag2_send, ag2_recv).wait_send()
        return c

    lax.fori_loop(1, n, drain, 0)
    for k in range(1, groups):
        group_copy(hot_ref, got_hot, k, hot_send, hot_recv).wait_send()
        group_copy(part1, got1, k, rs1_send, rs1_recv).wait_send()
    for k in range(1, groups):
        group_copy(part2, got2, k, rs2_send, rs2_recv).wait_recv()
    sums = combine(part2, got2)
    for b in range(blocks):
        raw = jnp.dot(sums[b], w2_ref[...], preferred_element_type=F32) + b2_ref[...]
        out_ref[b * size : (b + 1) * size, :] = raw.astype(BF16)
    for k in range(1, groups):
        group_copy(part2, got2, k, rs2_send, rs2_recv).wait_send()


def body(
    features,
    edge_tiles,
    tile_slot,
    tile_column,
    mirror_count,
    mirror_block,
    weight_first,
    bias_first,
    weight_second,
    bias_second,
):
    groups = lax.axis_size("group")
    n = lax.axis_size("member")
    total, size, _ = edge_tiles.shape
    rows, width = features.shape
    hidden = weight_first.shape[1]
    outs = weight_second.shape[1]
    blocks = rows // size
    cap = mirror_block.shape[2]
    slots = groups * cap
    columns = n * blocks
    counts = mirror_count[0]
    slot = tile_slot[0]
    dest = slot // cap
    count_of = jnp.sum(
        jnp.where(dest[:, None] == jnp.arange(groups)[None, :], counts[None, :], 0), axis=1
    )
    live = (slot % cap) < count_of
    key = jnp.where(live, slot * columns + tile_column[0], -1)
    order = jnp.arange(total, dtype=jnp.int32)
    same = (key[:, None] == key[None, :]) & (order[None, :] < order[:, None])
    prev = jnp.max(jnp.where(same, order[None, :], -1), axis=1)
    prev = jnp.where(prev < 0, total, prev)
    combos = jnp.arange(slots * columns, dtype=jnp.int32)
    last = jnp.max(jnp.where(key[None, :] == combos[:, None], order[None, :], -1), axis=1)
    last = jnp.where(last < 0, total, last)
    hot = (mirror_block[0][:, :, None] == jnp.arange(blocks)[None, None, :]) & (
        jnp.arange(cap)[None, :, None] < counts[:, None, None]
    )
    hot = jnp.broadcast_to(
        hot.reshape(groups, cap * blocks, 1).astype(F32), (groups, cap * blocks, width)
    )
    keep = slots * columns <= 2 * total
    pieces = 8 if total % 8 == 0 else 1
    vmem = pl.BlockSpec(memory_space=pltpu.VMEM)
    smem = pl.BlockSpec(memory_space=pltpu.SMEM)
    dma = pltpu.SemaphoreType.DMA
    return pl.pallas_call(
        functools.partial(kernel, n, groups, cap, keep),
        out_shape=jax.ShapeDtypeStruct((rows, outs), BF16),
        in_specs=[smem, smem, vmem, pl.BlockSpec(memory_space=pl.ANY)] + [vmem] * 5,
        out_specs=vmem,
        scratch_shapes=[
            pltpu.VMEM((total + 1, size, size), BF16),
            pltpu.VMEM((total + 1, size, size), F32),
            pltpu.VMEM((n if keep else 1, slots * size, rows), BF16),
            pltpu.VMEM((n, rows, width), BF16),
            pltpu.VMEM((n, rows, width), BF16),
            pltpu.VMEM((slots * size, width), F32),
            pltpu.VMEM((slots * size, hidden), F32),
            pltpu.VMEM((groups, cap * size, width), BF16),
            pltpu.VMEM((groups, cap * size, hidden), BF16),
            pltpu.VMEM((groups, cap * size, width), BF16),
            pltpu.VMEM((groups, cap * size, hidden), BF16),
            pltpu.VMEM((groups, cap * blocks, width), F32),
            pltpu.VMEM((rows, width), BF16),
            dma((pieces,)),
            dma((groups,)),
            dma((groups,)),
            dma((n,)),
            dma((n,)),
            dma((groups,)),
            dma((groups,)),
            dma((n,)),
            dma((n,)),
            dma((groups,)),
            dma((groups,)),
        ],
        compiler_params=pltpu.CompilerParams(
            collective_id=0, has_side_effects=True, vmem_limit_bytes=56 * 1024 * 1024
        ),
    )(
        prev,
        last,
        features,
        edge_tiles,
        hot,
        weight_first,
        bias_first.reshape(1, -1),
        weight_second,
        bias_second.reshape(1, -1),
    )


def solution(mesh):
    placed = (
        P(("group", "member"), None),
        P(("group", "member"), None, None),
        P(("group", "member"), None),
        P(("group", "member"), None),
        P(("group", "member"), None),
        P(("group", "member"), None, None),
        P(),
        P(),
        P(),
        P(),
    )
    return jax.shard_map(
        body, mesh=mesh, in_specs=placed, out_specs=P(("group", "member"), None), check_vma=False
    )
```

```python
import functools

import jax
import jax.numpy as jnp
from jax import lax
from jax.experimental import pallas as pl
from jax.experimental.pallas import tpu as pltpu
from jax.sharding import PartitionSpec as P

F32 = jnp.float32
BF16 = jnp.bfloat16


def kernel(
    outer,
    inner,
    groups,
    cap,
    keep,
    slot_ref,
    column_ref,
    count_ref,
    mirror_ref,
    feat_ref,
    tiles_ref,
    w1_ref,
    b1_ref,
    w2_ref,
    b2_ref,
    out_ref,
    tile_buf,
    run_buf,
    stage_buf,
    gather1,
    gather2,
    acc1,
    acc2,
    part1,
    part2,
    got1,
    got2,
    got_hot,
    own_sum,
    hot_ref,
    prev_vmem,
    last_vmem,
    prev_ref,
    last_ref,
    table_sem,
    tile_sem,
    hot_send,
    hot_recv,
    ag1_send,
    ag1_recv,
    rs1_send,
    rs1_recv,
    ag2_send,
    ag2_recv,
    rs2_send,
    rs2_recv,
):
    n = outer * inner
    me = lax.axis_index("member")
    me_outer, me_inner = me // inner, lax.rem(me, inner)
    g = lax.axis_index("group")
    total = tiles_ref.shape[0]
    size = tiles_ref.shape[1]
    rows = feat_ref.shape[0]
    blocks = rows // size
    slots = groups * cap
    columns = n * blocks
    pieces = tile_sem.shape[0]
    piece = total // pieces

    def tile_copy(i):
        span = pl.ds(i * piece, piece)
        return pltpu.make_async_copy(tiles_ref.at[span], tile_buf.at[span], tile_sem.at[i])

    def outer_copy(src, bank, j, send, recv, arriving=False):
        from_outer = lax.rem(me_outer + outer - j, outer)
        origin = from_outer * inner + me_inner
        to = lax.rem(me_outer + j, outer) * inner + me_inner
        return pltpu.make_async_remote_copy(
            src_ref=src,
            dst_ref=bank.at[origin if arriving else me],
            send_sem=send.at[j],
            recv_sem=recv.at[j],
            device_id={"member": to},
            device_id_type=pl.DeviceIdType.MESH,
        )

    def inner_copy(src, bank, j, hop, send, recv, arriving=False):
        from_outer = lax.rem(me_outer + outer - j, outer)
        from_inner = lax.rem(me_inner + inner - hop, inner)
        mine = from_outer * inner + me_inner
        origin = from_outer * inner + from_inner
        to = me_outer * inner + lax.rem(me_inner + hop, inner)
        at = outer + j * (inner - 1) + hop - 1
        return pltpu.make_async_remote_copy(
            src_ref=src if j == 0 else bank.at[mine],
            dst_ref=bank.at[origin if arriving else mine],
            send_sem=send.at[at],
            recv_sem=recv.at[at],
            device_id={"member": to},
            device_id_type=pl.DeviceIdType.MESH,
        )

    hops = sorted(range(1, outer), key=lambda j: (min(j, outer - j), j))

    def over_inner(do):
        def step(hop, c):
            do(hop)
            return c

        lax.fori_loop(1, inner, step, 0)

    def gather_start(src, bank, send, recv):
        over_inner(lambda hop: inner_copy(src, bank, 0, hop, send, recv).start())
        for j in hops:
            outer_copy(src, bank, j, send, recv).start()

    def forward(src, bank, j, send, recv):
        outer_copy(src, bank, j, send, recv, True).wait_recv()
        over_inner(lambda hop: inner_copy(src, bank, j, hop, send, recv).start())

    def gather_inner(src, bank, j, send, recv, use):
        def do(hop):
            inner_copy(src, bank, j, hop, send, recv, True).wait_recv()
            from_outer = lax.rem(me_outer + outer - j, outer)
            use(from_outer * inner + lax.rem(me_inner + inner - hop, inner))

        over_inner(do)

    def outer_origin(j):
        return lax.rem(me_outer + outer - j, outer) * inner + me_inner

    def gather_drain(src, bank, send, recv):
        for j in hops:
            outer_copy(src, bank, j, send, recv).wait_send()
        for j in range(outer):
            over_inner(lambda hop: inner_copy(src, bank, j, hop, send, recv).wait_send())

    def group_copy(bank, got, k, send, recv):
        to = lax.rem(g + k, groups)
        return pltpu.make_async_remote_copy(
            src_ref=bank.at[to],
            dst_ref=got.at[k],
            send_sem=send.at[k],
            recv_sem=recv.at[k],
            device_id={"group": to},
            device_id_type=pl.DeviceIdType.MESH,
        )

    for i in range(pieces):
        tile_copy(i).start()

    barrier = pltpu.get_barrier_semaphore()

    def greet_member(k, c):
        pl.semaphore_signal(
            barrier,
            inc=1,
            device_id={"member": lax.rem(me + k, n)},
            device_id_type=pl.DeviceIdType.MESH,
        )
        return c

    lax.fori_loop(1, n, greet_member, 0)
    for k in range(1, groups):
        pl.semaphore_signal(
            barrier,
            inc=1,
            device_id={"group": lax.rem(g + k, groups)},
            device_id_type=pl.DeviceIdType.MESH,
        )
    pl.semaphore_wait(barrier, n - 1 + groups - 1)

    ag1 = (feat_ref, gather1)
    sem1 = (ag1_send, ag1_recv)
    gather_start(*ag1, *sem1)

    for e in range(groups):
        shape = (cap * blocks, feat_ref.shape[1])
        line = lax.broadcasted_iota(jnp.int32, shape, 0)
        value = jnp.zeros(shape, F32)
        for c in range(cap):
            target = jnp.where(c < count_ref[0, e], c * blocks + mirror_ref[0, e, c], -1)
            value = jnp.where(line == target, 1.0, value)
        hot_ref[e] = value
    for k in range(1, groups):
        group_copy(hot_ref, got_hot, k, hot_send, hot_recv).start()

    slot = slot_ref[...]
    dest = slot // cap
    live = jnp.zeros(slot.shape, jnp.int32)
    for e in range(groups):
        live = jnp.where(dest == e, count_ref[0, e], live)
    key = jnp.where(slot - dest * cap < live, slot * columns + column_ref[...], -1)
    key_down = jnp.transpose(jnp.broadcast_to(key, (8, total)))[:, 0:1]
    earlier = lax.broadcasted_iota(jnp.int32, (total, total), 0)
    order = lax.broadcasted_iota(jnp.int32, (total, total), 1)
    same = (key_down == key) & (earlier < order)
    found = jnp.max(jnp.where(same, earlier, -1), axis=0, keepdims=True)
    prev_vmem[...] = jnp.where(found < 0, total, found)
    for i in range(0, slots * columns, total):
        found = jnp.max(
            jnp.where(key_down == order + i, earlier, -1), axis=0, keepdims=True
        )
        last_vmem[:, i : i + total] = jnp.where(found < 0, total, found)
    prev_copy = pltpu.make_async_copy(prev_vmem, prev_ref, table_sem.at[0])
    last_copy = pltpu.make_async_copy(last_vmem, last_ref, table_sem.at[1])
    prev_copy.start()
    last_copy.start()
    tile_buf[total] = jnp.zeros((size, size), BF16)
    run_buf[total] = jnp.zeros((size, size), F32)

    prev_copy.wait()
    last_copy.wait()

    def chain(t, c):
        value = tile_buf[t].astype(F32) + run_buf[prev_ref[0, t]]
        run_buf[t] = value
        tile_buf[t] = value.astype(BF16)
        return c

    for i in range(pieces):
        tile_copy(i).wait()
        lax.fori_loop(i * piece, (i + 1) * piece, chain, 0)
        if i % 2 == 1 and i // 2 < len(hops):
            forward(*ag1, hops[i // 2], *sem1)
    for j in hops[pieces // 2 :]:
        forward(*ag1, j, *sem1)

    def stage(origin, at):
        for s in range(slots):
            for b in range(blocks):
                stage_buf[at, s * size : (s + 1) * size, b * size : (b + 1) * size] = tile_buf[
                    last_ref[0, s * columns + origin * blocks + b]
                ]

    if keep:

        def stage_all(k, c):
            stage(k, k)
            return c

        lax.fori_loop(0, n, stage_all, 0)

    def place(origin):
        if keep:
            return origin
        stage(origin, 0)
        return 0

    def combine(part, got):
        sums = []
        for b in range(blocks):
            value = None
            for k in range(groups):
                hot = hot_ref[g] if k == 0 else got_hot[k]
                for c in range(cap):
                    block = (
                        part[g, c * size : (c + 1) * size, :]
                        if k == 0
                        else got[k, c * size : (c + 1) * size, :]
                    )
                    weight = hot[c * blocks + b : c * blocks + b + 1, :]
                    repeat = block.shape[1] // weight.shape[1]
                    if repeat > 1:
                        weight = jnp.concatenate([weight] * repeat, axis=1)
                    term = weight * block.astype(F32)
                    value = term if value is None else value + term
            sums.append(value.astype(BF16))
        return sums

    acc1[...] = jnp.dot(stage_buf[place(me)], feat_ref[...], preferred_element_type=F32)

    def first_layer(origin):
        at = place(origin)
        acc1[...] += jnp.dot(stage_buf[at], gather1[origin], preferred_element_type=F32)

    for j in hops:
        first_layer(outer_origin(j))
    for j in [0] + hops:
        gather_inner(*ag1, j, *sem1, first_layer)
    for e in range(groups):
        part1[e] = acc1[e * cap * size : (e + 1) * cap * size, :].astype(BF16)
    for k in range(1, groups):
        group_copy(part1, got1, k, rs1_send, rs1_recv).start()
    for k in range(1, groups):
        group_copy(hot_ref, got_hot, k, hot_send, hot_recv).wait_recv()
    for k in range(1, groups):
        group_copy(part1, got1, k, rs1_send, rs1_recv).wait_recv()
    sums = combine(part1, got1)
    for b in range(blocks):
        own_sum[b * size : (b + 1) * size, :] = sums[b]

    ag2 = (own_sum, gather2)
    sem2 = (ag2_send, ag2_recv)
    gather_start(*ag2, *sem2)

    def hidden_of(value):
        raw = jnp.dot(value, w1_ref[...], preferred_element_type=F32) + b1_ref[...]
        return jnp.maximum(raw, 0.0).astype(BF16)

    acc2[...] = jnp.dot(stage_buf[place(me)], hidden_of(own_sum[...]), preferred_element_type=F32)

    def second_layer(origin):
        at = place(origin)
        acc2[...] += jnp.dot(
            stage_buf[at], hidden_of(gather2[origin]), preferred_element_type=F32
        )

    waiting = []
    for j in hops:
        forward(*ag2, j, *sem2)
        for i in waiting:
            second_layer(outer_origin(i))
        waiting = [j]
        if j == hops[1]:
            gather_inner(*ag2, 0, *sem2, second_layer)
    for i in waiting:
        second_layer(outer_origin(i))
    for j in hops:
        gather_inner(*ag2, j, *sem2, second_layer)
    for e in range(groups):
        part2[e] = acc2[e * cap * size : (e + 1) * cap * size, :].astype(BF16)
    for k in range(1, groups):
        group_copy(part2, got2, k, rs2_send, rs2_recv).start()

    gather_drain(*ag1, *sem1)
    gather_drain(*ag2, *sem2)
    for k in range(1, groups):
        group_copy(hot_ref, got_hot, k, hot_send, hot_recv).wait_send()
        group_copy(part1, got1, k, rs1_send, rs1_recv).wait_send()
    for k in range(1, groups):
        group_copy(part2, got2, k, rs2_send, rs2_recv).wait_recv()
    sums = combine(part2, got2)
    for b in range(blocks):
        raw = jnp.dot(sums[b], w2_ref[...], preferred_element_type=F32) + b2_ref[...]
        out_ref[b * size : (b + 1) * size, :] = raw.astype(BF16)
    for k in range(1, groups):
        group_copy(part2, got2, k, rs2_send, rs2_recv).wait_send()


def body(
    features,
    edge_tiles,
    tile_slot,
    tile_column,
    mirror_count,
    mirror_block,
    weight_first,
    bias_first,
    weight_second,
    bias_second,
):
    groups = lax.axis_size("group")
    n = lax.axis_size("member")
    total, size, _ = edge_tiles.shape
    rows, width = features.shape
    hidden = weight_first.shape[1]
    outs = weight_second.shape[1]
    blocks = rows // size
    cap = mirror_block.shape[2]
    slots = groups * cap
    columns = n * blocks
    keep = slots * columns <= 2 * total
    pieces = 8 if total % 8 == 0 else 1
    outer = 4
    inner = n // outer
    vmem = pl.BlockSpec(memory_space=pltpu.VMEM)
    smem = pl.BlockSpec(memory_space=pltpu.SMEM)
    dma = pltpu.SemaphoreType.DMA
    return pl.pallas_call(
        functools.partial(kernel, outer, inner, groups, cap, keep),
        out_shape=jax.ShapeDtypeStruct((rows, outs), BF16),
        in_specs=[vmem, vmem, smem, smem, vmem, pl.BlockSpec(memory_space=pl.ANY)] + [vmem] * 4,
        out_specs=vmem,
        scratch_shapes=[
            pltpu.VMEM((total + 1, size, size), BF16),
            pltpu.VMEM((total + 1, size, size), F32),
            pltpu.VMEM((n if keep else 1, slots * size, rows), BF16),
            pltpu.VMEM((n, rows, width), BF16),
            pltpu.VMEM((n, rows, width), BF16),
            pltpu.VMEM((slots * size, width), F32),
            pltpu.VMEM((slots * size, hidden), F32),
            pltpu.VMEM((groups, cap * size, width), BF16),
            pltpu.VMEM((groups, cap * size, hidden), BF16),
            pltpu.VMEM((groups, cap * size, width), BF16),
            pltpu.VMEM((groups, cap * size, hidden), BF16),
            pltpu.VMEM((groups, cap * blocks, width), F32),
            pltpu.VMEM((rows, width), BF16),
            pltpu.VMEM((groups, cap * blocks, width), F32),
            pltpu.VMEM((1, total), jnp.int32),
            pltpu.VMEM((1, slots * columns), jnp.int32),
            pltpu.SMEM((1, total), jnp.int32),
            pltpu.SMEM((1, slots * columns), jnp.int32),
            dma((2,)),
            dma((pieces,)),
            dma((groups,)),
            dma((groups,)),
            dma((n,)),
            dma((n,)),
            dma((groups,)),
            dma((groups,)),
            dma((n,)),
            dma((n,)),
            dma((groups,)),
            dma((groups,)),
        ],
        compiler_params=pltpu.CompilerParams(
            collective_id=0, has_side_effects=True, vmem_limit_bytes=56 * 1024 * 1024
        ),
    )(
        tile_slot,
        tile_column,
        mirror_count,
        mirror_block,
        features,
        edge_tiles,
        weight_first,
        bias_first.reshape(1, -1),
        weight_second,
        bias_second.reshape(1, -1),
    )


def solution(mesh):
    placed = (
        P(("group", "member"), None),
        P(("group", "member"), None, None),
        P(("group", "member"), None),
        P(("group", "member"), None),
        P(("group", "member"), None),
        P(("group", "member"), None, None),
        P(),
        P(),
        P(),
        P(),
    )
    return jax.shard_map(
        body, mesh=mesh, in_specs=placed, out_specs=P(("group", "member"), None), check_vma=False
    )
```

```python
import functools

import jax
import jax.numpy as jnp
from jax import lax
from jax.experimental import pallas as pl
from jax.experimental.pallas import tpu as pltpu
from jax.sharding import PartitionSpec as P

F32 = jnp.float32
BF16 = jnp.bfloat16


def kernel(
    outer,
    inner,
    groups,
    cap,
    keep,
    slot_ref,
    column_ref,
    count_ref,
    mirror_ref,
    feat_ref,
    tiles_ref,
    w1_ref,
    b1_ref,
    w2_ref,
    b2_ref,
    out_ref,
    tile_buf,
    run_buf,
    stage_buf,
    gather1,
    gather2,
    acc1,
    acc2,
    part1,
    part2,
    got1,
    got2,
    got_hot,
    own_sum,
    hot_ref,
    prev_vmem,
    last_vmem,
    prev_ref,
    last_ref,
    table_sem,
    tile_sem,
    hot_send,
    hot_recv,
    ag1_send,
    ag1_recv,
    rs1_send,
    rs1_recv,
    ag2_send,
    ag2_recv,
    rs2_send,
    rs2_recv,
):
    n = outer * inner
    me = lax.axis_index("member")
    me_outer, me_inner = me // inner, lax.rem(me, inner)
    g = lax.axis_index("group")
    total = tiles_ref.shape[0]
    size = tiles_ref.shape[1]
    rows = feat_ref.shape[0]
    blocks = rows // size
    slots = groups * cap
    columns = n * blocks
    pieces = tile_sem.shape[0]
    piece = total // pieces

    def tile_copy(i):
        span = pl.ds(i * piece, piece)
        return pltpu.make_async_copy(tiles_ref.at[span], tile_buf.at[span], tile_sem.at[i])

    def outer_copy(src, bank, j, send, recv, arriving=False):
        from_outer = lax.rem(me_outer + outer - j, outer)
        origin = from_outer * inner + me_inner
        to = lax.rem(me_outer + j, outer) * inner + me_inner
        return pltpu.make_async_remote_copy(
            src_ref=src,
            dst_ref=bank.at[origin if arriving else me],
            send_sem=send.at[j],
            recv_sem=recv.at[j],
            device_id={"member": to},
            device_id_type=pl.DeviceIdType.MESH,
        )

    def inner_copy(src, bank, j, hop, send, recv, arriving=False):
        from_outer = lax.rem(me_outer + outer - j, outer)
        from_inner = lax.rem(me_inner + inner - hop, inner)
        mine = from_outer * inner + me_inner
        origin = from_outer * inner + from_inner
        to = me_outer * inner + lax.rem(me_inner + hop, inner)
        at = outer + j * (inner - 1) + hop - 1
        return pltpu.make_async_remote_copy(
            src_ref=src if j == 0 else bank.at[mine],
            dst_ref=bank.at[origin if arriving else mine],
            send_sem=send.at[at],
            recv_sem=recv.at[at],
            device_id={"member": to},
            device_id_type=pl.DeviceIdType.MESH,
        )

    hops = sorted(range(1, outer), key=lambda j: (min(j, outer - j), j))

    def over_inner(do):
        def step(hop, c):
            do(hop)
            return c

        lax.fori_loop(1, inner, step, 0)

    def gather_start(src, bank, send, recv):
        over_inner(lambda hop: inner_copy(src, bank, 0, hop, send, recv).start())
        for j in hops:
            outer_copy(src, bank, j, send, recv).start()

    def forward(src, bank, j, send, recv):
        outer_copy(src, bank, j, send, recv, True).wait_recv()
        over_inner(lambda hop: inner_copy(src, bank, j, hop, send, recv).start())

    def gather_inner(src, bank, j, send, recv, use):
        def do(hop):
            inner_copy(src, bank, j, hop, send, recv, True).wait_recv()
            from_outer = lax.rem(me_outer + outer - j, outer)
            use(from_outer * inner + lax.rem(me_inner + inner - hop, inner))

        over_inner(do)

    def outer_origin(j):
        return lax.rem(me_outer + outer - j, outer) * inner + me_inner

    def gather_drain(src, bank, send, recv):
        for j in hops:
            outer_copy(src, bank, j, send, recv).wait_send()
        for j in range(outer):
            over_inner(lambda hop: inner_copy(src, bank, j, hop, send, recv).wait_send())

    def group_copy(bank, got, k, send, recv):
        to = lax.rem(g + k, groups)
        return pltpu.make_async_remote_copy(
            src_ref=bank.at[to],
            dst_ref=got.at[k],
            send_sem=send.at[k],
            recv_sem=recv.at[k],
            device_id={"group": to},
            device_id_type=pl.DeviceIdType.MESH,
        )

    for i in range(pieces):
        tile_copy(i).start()

    barrier = pltpu.get_barrier_semaphore()

    def greet_member(k, c):
        pl.semaphore_signal(
            barrier,
            inc=1,
            device_id={"member": lax.rem(me + k, n)},
            device_id_type=pl.DeviceIdType.MESH,
        )
        return c

    lax.fori_loop(1, n, greet_member, 0)
    for k in range(1, groups):
        pl.semaphore_signal(
            barrier,
            inc=1,
            device_id={"group": lax.rem(g + k, groups)},
            device_id_type=pl.DeviceIdType.MESH,
        )
    pl.semaphore_wait(barrier, n - 1 + groups - 1)

    ag1 = (feat_ref, gather1)
    sem1 = (ag1_send, ag1_recv)
    gather_start(*ag1, *sem1)

    for e in range(groups):
        shape = (cap * blocks, feat_ref.shape[1])
        line = lax.broadcasted_iota(jnp.int32, shape, 0)
        value = jnp.zeros(shape, F32)
        for c in range(cap):
            target = jnp.where(c < count_ref[0, e], c * blocks + mirror_ref[0, e, c], -1)
            value = jnp.where(line == target, 1.0, value)
        hot_ref[e] = value
    for k in range(1, groups):
        group_copy(hot_ref, got_hot, k, hot_send, hot_recv).start()

    slot = slot_ref[...]
    dest = slot // cap
    live = jnp.zeros(slot.shape, jnp.int32)
    for e in range(groups):
        live = jnp.where(dest == e, count_ref[0, e], live)
    key = jnp.where(slot - dest * cap < live, slot * columns + column_ref[...], -1)
    key_down = jnp.transpose(jnp.broadcast_to(key, (8, total)))[:, 0:1]
    earlier = lax.broadcasted_iota(jnp.int32, (total, total), 0)
    order = lax.broadcasted_iota(jnp.int32, (total, total), 1)
    same = (key_down == key) & (earlier < order)
    found = jnp.max(jnp.where(same, earlier, -1), axis=0, keepdims=True)
    prev_vmem[...] = jnp.where(found < 0, total, found)
    for i in range(0, slots * columns, total):
        found = jnp.max(
            jnp.where(key_down == order + i, earlier, -1), axis=0, keepdims=True
        )
        last_vmem[:, i : i + total] = jnp.where(found < 0, total, found)
    prev_copy = pltpu.make_async_copy(prev_vmem, prev_ref, table_sem.at[0])
    last_copy = pltpu.make_async_copy(last_vmem, last_ref, table_sem.at[1])
    prev_copy.start()
    last_copy.start()
    tile_buf[total] = jnp.zeros((size, size), BF16)
    run_buf[total] = jnp.zeros((size, size), F32)

    prev_copy.wait()
    last_copy.wait()

    def chain(t, c):
        value = tile_buf[t].astype(F32) + run_buf[prev_ref[0, t]]
        run_buf[t] = value
        tile_buf[t] = value.astype(BF16)
        return c

    for i in range(pieces):
        tile_copy(i).wait()
        lax.fori_loop(i * piece, (i + 1) * piece, chain, 0, unroll=4)
        if i % 2 == 1 and i // 2 < len(hops):
            forward(*ag1, hops[i // 2], *sem1)
    for j in hops[pieces // 2 :]:
        forward(*ag1, j, *sem1)

    def stage(origin, at):
        for s in range(slots):
            for b in range(blocks):
                stage_buf[at, s * size : (s + 1) * size, b * size : (b + 1) * size] = tile_buf[
                    last_ref[0, s * columns + origin * blocks + b]
                ]

    if keep:

        def stage_all(k, c):
            stage(k, k)
            return c

        lax.fori_loop(0, n, stage_all, 0)

    def place(origin):
        if keep:
            return origin
        stage(origin, 0)
        return 0

    def combine(part, got):
        sums = []
        for b in range(blocks):
            value = None
            for k in range(groups):
                hot = hot_ref[g] if k == 0 else got_hot[k]
                for c in range(cap):
                    block = (
                        part[g, c * size : (c + 1) * size, :]
                        if k == 0
                        else got[k, c * size : (c + 1) * size, :]
                    )
                    weight = hot[c * blocks + b : c * blocks + b + 1, :]
                    repeat = block.shape[1] // weight.shape[1]
                    if repeat > 1:
                        weight = jnp.concatenate([weight] * repeat, axis=1)
                    term = weight * block.astype(F32)
                    value = term if value is None else value + term
            sums.append(value.astype(BF16))
        return sums

    acc1[...] = jnp.dot(stage_buf[place(me)], feat_ref[...], preferred_element_type=F32)

    def first_layer(origin):
        at = place(origin)
        acc1[...] += jnp.dot(stage_buf[at], gather1[origin], preferred_element_type=F32)

    for j in hops:
        first_layer(outer_origin(j))
    for j in [0] + hops:
        gather_inner(*ag1, j, *sem1, first_layer)
    for e in range(groups):
        part1[e] = acc1[e * cap * size : (e + 1) * cap * size, :].astype(BF16)
    for k in range(1, groups):
        group_copy(part1, got1, k, rs1_send, rs1_recv).start()
    for k in range(1, groups):
        group_copy(hot_ref, got_hot, k, hot_send, hot_recv).wait_recv()
    for k in range(1, groups):
        group_copy(part1, got1, k, rs1_send, rs1_recv).wait_recv()
    sums = combine(part1, got1)
    for b in range(blocks):
        own_sum[b * size : (b + 1) * size, :] = sums[b]

    ag2 = (own_sum, gather2)
    sem2 = (ag2_send, ag2_recv)
    gather_start(*ag2, *sem2)

    def hidden_of(value):
        raw = jnp.dot(value, w1_ref[...], preferred_element_type=F32) + b1_ref[...]
        return jnp.maximum(raw, 0.0).astype(BF16)

    acc2[...] = jnp.dot(stage_buf[place(me)], hidden_of(own_sum[...]), preferred_element_type=F32)

    def second_layer(origin):
        at = place(origin)
        acc2[...] += jnp.dot(
            stage_buf[at], hidden_of(gather2[origin]), preferred_element_type=F32
        )

    waiting = []
    for j in hops:
        forward(*ag2, j, *sem2)
        for i in waiting:
            second_layer(outer_origin(i))
        waiting = [j]
        if j == hops[1]:
            gather_inner(*ag2, 0, *sem2, second_layer)
    for i in waiting:
        second_layer(outer_origin(i))
    for j in hops:
        gather_inner(*ag2, j, *sem2, second_layer)
    for e in range(groups):
        part2[e] = acc2[e * cap * size : (e + 1) * cap * size, :].astype(BF16)
    for k in range(1, groups):
        group_copy(part2, got2, k, rs2_send, rs2_recv).start()

    gather_drain(*ag1, *sem1)
    gather_drain(*ag2, *sem2)
    for k in range(1, groups):
        group_copy(hot_ref, got_hot, k, hot_send, hot_recv).wait_send()
        group_copy(part1, got1, k, rs1_send, rs1_recv).wait_send()
    for k in range(1, groups):
        group_copy(part2, got2, k, rs2_send, rs2_recv).wait_recv()
    sums = combine(part2, got2)
    for b in range(blocks):
        raw = jnp.dot(sums[b], w2_ref[...], preferred_element_type=F32) + b2_ref[...]
        out_ref[b * size : (b + 1) * size, :] = raw.astype(BF16)
    for k in range(1, groups):
        group_copy(part2, got2, k, rs2_send, rs2_recv).wait_send()


def body(
    features,
    edge_tiles,
    tile_slot,
    tile_column,
    mirror_count,
    mirror_block,
    weight_first,
    bias_first,
    weight_second,
    bias_second,
):
    groups = lax.axis_size("group")
    n = lax.axis_size("member")
    total, size, _ = edge_tiles.shape
    rows, width = features.shape
    hidden = weight_first.shape[1]
    outs = weight_second.shape[1]
    blocks = rows // size
    cap = mirror_block.shape[2]
    slots = groups * cap
    columns = n * blocks
    keep = slots * columns <= 2 * total
    pieces = 8 if total % 8 == 0 else 1
    outer = 4
    inner = n // outer
    vmem = pl.BlockSpec(memory_space=pltpu.VMEM)
    smem = pl.BlockSpec(memory_space=pltpu.SMEM)
    dma = pltpu.SemaphoreType.DMA
    return pl.pallas_call(
        functools.partial(kernel, outer, inner, groups, cap, keep),
        out_shape=jax.ShapeDtypeStruct((rows, outs), BF16),
        in_specs=[vmem, vmem, smem, smem, vmem, pl.BlockSpec(memory_space=pl.ANY)] + [vmem] * 4,
        out_specs=vmem,
        scratch_shapes=[
            pltpu.VMEM((total + 1, size, size), BF16),
            pltpu.VMEM((total + 1, size, size), F32),
            pltpu.VMEM((n if keep else 1, slots * size, rows), BF16),
            pltpu.VMEM((n, rows, width), BF16),
            pltpu.VMEM((n, rows, width), BF16),
            pltpu.VMEM((slots * size, width), F32),
            pltpu.VMEM((slots * size, hidden), F32),
            pltpu.VMEM((groups, cap * size, width), BF16),
            pltpu.VMEM((groups, cap * size, hidden), BF16),
            pltpu.VMEM((groups, cap * size, width), BF16),
            pltpu.VMEM((groups, cap * size, hidden), BF16),
            pltpu.VMEM((groups, cap * blocks, width), F32),
            pltpu.VMEM((rows, width), BF16),
            pltpu.VMEM((groups, cap * blocks, width), F32),
            pltpu.VMEM((1, total), jnp.int32),
            pltpu.VMEM((1, slots * columns), jnp.int32),
            pltpu.SMEM((1, total), jnp.int32),
            pltpu.SMEM((1, slots * columns), jnp.int32),
            dma((2,)),
            dma((pieces,)),
            dma((groups,)),
            dma((groups,)),
            dma((n,)),
            dma((n,)),
            dma((groups,)),
            dma((groups,)),
            dma((n,)),
            dma((n,)),
            dma((groups,)),
            dma((groups,)),
        ],
        compiler_params=pltpu.CompilerParams(
            collective_id=0, has_side_effects=True, vmem_limit_bytes=56 * 1024 * 1024
        ),
    )(
        tile_slot,
        tile_column,
        mirror_count,
        mirror_block,
        features,
        edge_tiles,
        weight_first,
        bias_first.reshape(1, -1),
        weight_second,
        bias_second.reshape(1, -1),
    )


def solution(mesh):
    placed = (
        P(("group", "member"), None),
        P(("group", "member"), None, None),
        P(("group", "member"), None),
        P(("group", "member"), None),
        P(("group", "member"), None),
        P(("group", "member"), None, None),
        P(),
        P(),
        P(),
        P(),
    )
    return jax.shard_map(
        body, mesh=mesh, in_specs=placed, out_specs=P(("group", "member"), None), check_vma=False
    )
```
